32 devices in a mesh: trial: 4 (over z), row: 8 (over y, x, core).
Axes of the slice: x: 2, y: 2, z: 4, core: 2. Of those that a mesh axis runs over, the one named last changes fastest.
Arguments:
- phase_map: float32 [4096, 512], P('row'), may hold values from -3.140625 to 3.140625
- target: float32 [4096, 512], P('row'), may hold values from 0 to 2
- distance: float32 [4], P('trial'), may hold values from 0.25 to 1
- etch_class: int32 [4, 32, 4], P('trial', 'row'), may hold values from 0 to 3
- class_offset: float32 [4], replicated, may hold values from -0.6 to 0.6
- aperture_start: int32 [4], replicated, may hold values from 0 to 7
- aperture_stop: int32 [4], replicated, may hold values from 25 to 32
Outputs:
- phase_grad: float32 [4096, 512], P('row', 'trial')
The draws below stay inside these ranges and needn't reach their ends.
Inputs may be any that keep to these rules, and one draw needn't show every extreme that they name: `etch_class`: etch bias classes.
All inputs are finite; a program needn't handle non-finite values.
Results may differ from the reference program's by a relative error of at most 0.02.
Values may be sent and summed in bfloat16 or wider, within the bound.
A program may use at most 64 MiB of HBM per device.

```python
import jax
import jax.numpy as jnp
from jax import lax

W = 512
ROWS_DEV = 512
BLK = 128
CLASSES = 4
KEEP = 256
N = 4096
NB = 32
WB = 4
TRIALS = 4
N_ROW = 8


def touch_ends(array, own_key, smallest, largest):
    index_at = [jax.random.randint(jax.random.fold_in(own_key, axis), (), 0, length) for axis, length in enumerate(array.shape)]
    longest = array.shape.index(max(array.shape))
    beside = index_at[:longest] + [(index_at[longest] + 1) % array.shape[longest]] + index_at[longest + 1:]
    return array.at[tuple(index_at)].set(smallest).at[tuple(beside)].set(largest)


def block_levels(key, dims, cuts, smallest, high):
    gain = 1.0
    for position, blocks in cuts:
        draws = jax.random.uniform(jax.random.fold_in(jax.random.fold_in(key, 6), position), (blocks,), jnp.float32, smallest / len(cuts), high / len(cuts))
        gain = gain * jnp.repeat(jnp.exp(draws), dims[position] // blocks).reshape((-1,) + (1,) * (len(dims) - 1 - position))
    return gain


def setup_inputs(seed: int = 0) -> dict:
    arg_keys = jax.random.split(jax.random.key(seed), 8)
    return {
        "phase_map": jnp.clip(jax.random.uniform(arg_keys[0], (N, W), jnp.float32, -3.140625, 3.140625), -3.140625, 3.140625),
        "target": jnp.clip(2.0 * jax.random.uniform(arg_keys[1], (N, W), jnp.float32) ** block_levels(arg_keys[1], (N, W), ((0, 8),), -0.2, 0.2), 0.0, 2.0),
        "distance": jnp.clip(0.25 + 0.75 * jax.random.uniform(arg_keys[2], (TRIALS,), jnp.float32) ** block_levels(arg_keys[2], (TRIALS,), ((0, 4),), -0.2, 0.2), 0.25, 1.0),
        "etch_class": touch_ends(jax.random.randint(arg_keys[3], (TRIALS, NB, WB), 0, CLASSES), jax.random.fold_in(arg_keys[3], 1), 0, CLASSES - 1).astype(jnp.int32),
        "class_offset": jnp.clip(jax.random.uniform(arg_keys[4], (CLASSES,), jnp.float32, -0.6, 0.6), -0.6, 0.6),
        "aperture_start": touch_ends(jax.random.randint(arg_keys[5], (WB,), 0, NB // 4), jax.random.fold_in(arg_keys[5], 1), 0, (NB // 4) - 1).astype(jnp.int32),
        "aperture_stop": touch_ends(jax.random.randint(arg_keys[6], (WB,), 3 * NB // 4 + 1, NB + 1), jax.random.fold_in(arg_keys[6], 1), 3 * NB // 4 + 1, NB).astype(jnp.int32),
    }


HIGHEST_PRECISION = lax.Precision.HIGHEST


def cosine_pair(numer, denom):
    angle = (-2.0 * jnp.pi / denom) * numer.astype(jnp.float32)
    return jnp.cos(angle), jnp.sin(angle)


def column_tables(width, kept):
    columns = jnp.arange(width, dtype=jnp.int32)
    freqs = jnp.arange(kept, dtype=jnp.int32) - kept // 2
    table_real, table_imag = cosine_pair(jnp.mod(columns[:, None] * freqs[None, :], width), width)
    table_real = table_real.astype(jnp.bfloat16)
    table_imag = table_imag.astype(jnp.bfloat16)
    forward = jnp.concatenate([jnp.concatenate([table_real, table_imag], 1), jnp.concatenate([-table_imag, table_real], 1)], 0)
    backward = jnp.concatenate([jnp.concatenate([table_real.T, -table_imag.T], 1), jnp.concatenate([table_imag.T, table_real.T], 1)], 0)
    return forward, backward


def block_tables(height):
    places = jnp.arange(height, dtype=jnp.int32)
    table_real, table_imag = cosine_pair(jnp.mod(places[:, None] * places[None, :], height), height)
    table_real = table_real.astype(jnp.bfloat16)
    table_imag = table_imag.astype(jnp.bfloat16)
    forward = jnp.concatenate([jnp.concatenate([table_real, -table_imag], 1), jnp.concatenate([table_imag, table_real], 1)], 0)
    backward = jnp.concatenate([jnp.concatenate([table_real, table_imag], 1), jnp.concatenate([-table_imag, table_real], 1)], 0)
    return forward, backward


def transfer_phase(signed, across, dist, global_rows, width):
    row_freq = signed.astype(jnp.float32)
    col_freq = across.astype(jnp.float32)
    theta = (-jnp.pi * dist) * (row_freq * row_freq * (1.0 / global_rows) + col_freq * col_freq * (global_rows / (width * width)))
    return jnp.cos(theta), jnp.sin(theta)


def small_einsum(form, table, values):
    return jnp.einsum(form, table, values, precision=HIGHEST_PRECISION)


def reference(phase_map, target, distance, etch_class, class_offset, aperture_start, aperture_stop):
    col_fwd, col_back = column_tables(W, KEEP)
    blk_fwd, blk_back = block_tables(ROWS_DEV)
    group_ids = jnp.arange(N_ROW, dtype=jnp.int32)
    small_real, small_imag = cosine_pair(jnp.mod(group_ids[:, None] * group_ids[None, :], N_ROW), N_ROW)
    local_rows = jnp.arange(ROWS_DEV, dtype=jnp.int32)
    twist_real, twist_imag = cosine_pair(jnp.mod(group_ids[:, None] * local_rows[None, :], N), N)
    twist_real = twist_real[:, :, None]
    twist_imag = twist_imag[:, :, None]
    freq_rows = group_ids[:, None, None] + N_ROW * local_rows[None, :, None]
    signed = jnp.mod(freq_rows + N // 2, N) - N // 2
    across = (jnp.arange(KEEP, dtype=jnp.int32) - KEEP // 2)[None, None, :]
    row_block = jnp.arange(N, dtype=jnp.int32) // BLK
    col_block = jnp.arange(W, dtype=jnp.int32) // BLK
    inside = (row_block[:, None] >= aperture_start[col_block][None, :]) & (row_block[:, None] < aperture_stop[col_block][None, :])
    aperture_mask = inside.astype(jnp.float32)

    def propagate(field_real, field_imag, filter_real, filter_imag):
        columns = jnp.dot(jnp.concatenate([field_real, field_imag], 1), col_fwd, preferred_element_type=jnp.float32).astype(jnp.bfloat16)
        cols_real = columns[:, :KEEP].reshape(N_ROW, ROWS_DEV, KEEP).astype(jnp.float32)
        cols_imag = columns[:, KEEP:].reshape(N_ROW, ROWS_DEV, KEEP).astype(jnp.float32)
        mixed_real = small_einsum("kp,plc->klc", small_real, cols_real) - small_einsum("kp,plc->klc", small_imag, cols_imag)
        mixed_imag = small_einsum("kp,plc->klc", small_real, cols_imag) + small_einsum("kp,plc->klc", small_imag, cols_real)
        turned_real = (mixed_real * twist_real - mixed_imag * twist_imag).astype(jnp.bfloat16)
        turned_imag = (mixed_real * twist_imag + mixed_imag * twist_real).astype(jnp.bfloat16)
        stacked = jnp.concatenate([turned_real, turned_imag], 1).astype(jnp.float32)
        spectrum = small_einsum("ml,klc->kmc", blk_fwd.astype(jnp.float32), stacked)
        spec_real = spectrum[:, :ROWS_DEV]
        spec_imag = spectrum[:, ROWS_DEV:]
        filtered_real = (spec_real * filter_real - spec_imag * filter_imag).astype(jnp.bfloat16)
        filtered_imag = (spec_real * filter_imag + spec_imag * filter_real).astype(jnp.bfloat16)
        stacked = jnp.concatenate([filtered_real, filtered_imag], 1).astype(jnp.float32)
        unmixed = small_einsum("ml,klc->kmc", blk_back.astype(jnp.float32), stacked)
        unmixed_real = unmixed[:, :ROWS_DEV]
        unmixed_imag = unmixed[:, ROWS_DEV:]
        returned_real = (unmixed_real * twist_real + unmixed_imag * twist_imag).astype(jnp.bfloat16).astype(jnp.float32)
        returned_imag = (unmixed_imag * twist_real - unmixed_real * twist_imag).astype(jnp.bfloat16).astype(jnp.float32)
        near_real = (small_einsum("kp,klc->plc", small_real, returned_real) + small_einsum("kp,klc->plc", small_imag, returned_imag)) * (1.0 / N)
        near_imag = (small_einsum("kp,klc->plc", small_real, returned_imag) - small_einsum("kp,klc->plc", small_imag, returned_real)) * (1.0 / N)
        near = jnp.concatenate([near_real.reshape(N, KEEP), near_imag.reshape(N, KEEP)], 1).astype(jnp.bfloat16)
        result = jnp.dot(near, col_back, preferred_element_type=jnp.float32) * (1.0 / W)
        return result[:, :W], result[:, W:]

    def trial_step(total, per_trial):
        dist, classes = per_trial
        offsets = class_offset[classes]
        offset_map = jnp.repeat(jnp.repeat(offsets, BLK, 0), BLK, 1)
        angle_map = phase_map + offset_map
        lens_real = aperture_mask * jnp.cos(angle_map)
        lens_imag = aperture_mask * jnp.sin(angle_map)
        filter_real, filter_imag = transfer_phase(signed, across, dist, N, W)
        focal_real, focal_imag = propagate(lens_real.astype(jnp.bfloat16), lens_imag.astype(jnp.bfloat16), filter_real, filter_imag)
        residual = focal_real * focal_real + focal_imag * focal_imag - target
        back_real, back_imag = propagate((residual * focal_real).astype(jnp.bfloat16), (residual * focal_imag).astype(jnp.bfloat16), filter_real, -filter_imag)
        gradient = 2.0 * (lens_real * back_imag - lens_imag * back_real)
        return total + gradient, None

    total, _ = lax.scan(trial_step, jnp.zeros((N, W), jnp.float32), (distance, etch_class))
    return total
```

```python
import math

import jax
import jax.numpy as jnp
import numpy as np
from jax import lax
from jax.experimental import pallas as pl
from jax.experimental.pallas import tpu as pltpu
from jax.sharding import PartitionSpec as P

BLK = 128
LANES = 128
F32 = jnp.float32
BF16 = jnp.bfloat16
MESH = pl.DeviceIdType.MESH
MAGIC = 12582912.0


def even_fit(func, degree):
    cheb = np.polynomial.chebyshev.Chebyshev.interpolate(func, degree, domain=[0.0, 0.25])
    return [float(c) for c in cheb.convert(kind=np.polynomial.Polynomial).coef]


COS_FIT = even_fit(lambda z: np.cos(np.pi * np.sqrt(z)), 6)
SIN_FIT = even_fit(lambda z: np.pi * np.sinc(np.sqrt(z)), 5)


def horner(coefs, z):
    total = jnp.full_like(z, coefs[-1])
    for c in coefs[-2::-1]:
        total = total * z + c
    return total


def nearest(u):
    return (u + MAGIC) - MAGIC


def turn(u):
    whole = nearest(u)
    rest = u - whole
    z = rest * rest
    return horner(COS_FIT, z), rest * horner(SIN_FIT, z), whole


def cos_sin_pi(u):
    cos, sin, whole = turn(u)
    half = whole * 0.5
    odd = half - nearest(half)
    sign = 1.0 - 8.0 * (odd * odd)
    return cos * sign, sin * sign


def scale_turn(re, im, k, n, sign):
    if k == 0:
        return re, im
    if 4 * k == n:
        return (-im, re) if sign > 0 else (im, -re)
    c = math.cos(2 * math.pi * k / n)
    s = sign * math.sin(2 * math.pi * k / n)
    if 8 * k == n:
        return ((re - im) * c, (re + im) * c) if sign > 0 else ((re + im) * c, (im - re) * c)
    return re * c - im * s, re * s + im * c


def small_dft(values, sign):
    n = len(values)
    if n == 1:
        return values
    even = small_dft(values[0::2], sign)
    odd = small_dft(values[1::2], sign)
    low, high = [], []
    for k in range(n // 2):
        re, im = scale_turn(*odd[k], k, n, sign)
        low.append((even[k][0] + re, even[k][1] + im))
        high.append((even[k][0] - re, even[k][1] - im))
    return low + high


def tables(height, width, kept, groups, chunks):
    slim = kept // groups
    part = slim // chunks
    cols = np.arange(width)
    freqs = np.arange(kept) - kept // 2
    angle = -2.0 * np.pi / width * np.mod(cols[:, None] * freqs[None, :], width)
    re = np.cos(angle).T.reshape(groups, chunks, part, width)
    im = np.sin(angle).T.reshape(groups, chunks, part, width)
    rows_re = np.concatenate([re, -im], 3)
    rows_im = np.concatenate([im, re], 3)
    forward = np.stack([rows_re, rows_im], 2)
    forward = forward.transpose(1, 0, 2, 3, 4).reshape(2 * kept, 2 * width)
    places = np.arange(height)
    angle = -2.0 * np.pi / height * np.mod(places[:, None] * places[None, :], height)
    blk = np.stack([np.cos(angle), np.sin(angle)])
    total = height * groups
    angle = -2.0 * np.pi / total * np.mod(np.arange(groups)[:, None] * places[None, :], total)
    twist = np.stack([np.cos(angle), np.sin(angle)])
    as_bf16 = lambda a: jnp.asarray(a.astype(np.float32).astype(BF16))
    return as_bf16(forward), as_bf16(forward.T), as_bf16(blk), jnp.asarray(twist.astype(np.float32))


def kernel(
    dims,
    dist_ref,
    class_ref,
    level_ref,
    start_ref,
    stop_ref,
    phase_ref,
    target_ref,
    fwd_ref,
    back_ref,
    blk_ref,
    twist_ref,
    out_ref,
    lens,
    field,
    target_t,
    rowf,
    acc,
    packed,
    prod,
    send,
    recv,
    gsend,
    grecv,
    send_sem,
    recv_sem,
    gsend_sem,
    grecv_sem,
):
    groups, trials, height, width, kept, chunks = dims
    slim = kept // groups
    part = slim // chunks
    side = 2 * part
    half = groups * part
    span = 2 * kept // chunks
    total = height * groups
    me = lax.axis_index("row")
    mine = lax.axis_index("trial")
    lane_chunks = height // LANES

    barrier = pltpu.get_barrier_semaphore()
    for r in range(1, groups):
        pl.semaphore_signal(
            barrier, inc=1, device_id=(mine, lax.rem(me + r, groups)), device_id_type=MESH
        )
    for r in range(1, trials):
        pl.semaphore_signal(
            barrier, inc=1, device_id=(lax.rem(mine + r, trials), me), device_id_type=MESH
        )

    row_blocks = height // BLK
    col_blocks = width // BLK

    def lens_block(b, carry):
        cb = b // row_blocks
        rb = b % row_blocks
        rows = pl.ds(pl.multiple_of(rb * BLK, BLK), BLK)
        cols = pl.ds(pl.multiple_of(cb * BLK, BLK), BLK)
        offset = level_ref[class_ref[0, rb, cb]]
        where = me * row_blocks + rb
        inside = jnp.where(
            jnp.logical_and(where >= start_ref[cb], where < stop_ref[cb]), 1.0, 0.0
        ).astype(F32)
        angle = phase_ref[rows, cols].T + offset
        cos, sin, whole = turn(angle * (1.0 / math.pi))
        sign = inside - (2.0 * inside) * (whole * whole)
        re = cos * sign
        im = sin * sign
        low = pl.ds(pl.multiple_of(width + cb * BLK, BLK), BLK)
        lens[cols, rows] = re
        lens[low, rows] = im
        field[cols, rows] = re.astype(BF16)
        field[low, rows] = im.astype(BF16)
        return carry

    lax.fori_loop(0, row_blocks * col_blocks, lens_block, 0)

    def copy_to(slot, r):
        to = lax.rem(me + r, groups)
        return pltpu.make_async_remote_copy(
            src_ref=send.at[slot, to],
            dst_ref=recv.at[slot, me],
            send_sem=send_sem.at[slot, r],
            recv_sem=recv_sem.at[slot, r],
            device_id=(mine, to),
            device_id_type=MESH,
        )

    def exchange(slot):
        for r in range(1, groups):
            copy_to(slot, r).start()
        recv[slot, me] = send[slot, me]

    def arrive(slot):
        for r in range(1, groups):
            copy_to(slot, r).wait_recv()

    def columns(slot, q):
        made = jnp.dot(
            fwd_ref[q * span : (q + 1) * span, :], field[...], preferred_element_type=F32
        )
        send[slot] = made.astype(BF16).reshape(groups, side, height)

    def middle(slot_in, slot_out, q, conj):
        arrive(slot_in)

        def mix(n, carry):
            at = pl.ds(pl.multiple_of(n * LANES, LANES), LANES)
            values = []
            for p in range(groups):
                both = recv[slot_in, p, :, at].astype(F32)
                values.append((both[:part], both[part:]))
            for k, (re, im) in enumerate(small_dft(values, -1)):
                t_re = twist_ref[0, k : k + 1, at]
                t_im = twist_ref[1, k : k + 1, at]
                packed[k * part : (k + 1) * part, at] = (re * t_re - im * t_im).astype(BF16)
                packed[half + k * part : half + (k + 1) * part, at] = (
                    re * t_im + im * t_re
                ).astype(BF16)
            return carry

        lax.fori_loop(0, lane_chunks, mix, 0)
        prod[0] = jnp.dot(packed[...], blk_ref[0], preferred_element_type=F32)
        prod[1] = jnp.dot(packed[...], blk_ref[1], preferred_element_type=F32)
        across = (
            lax.broadcasted_iota(jnp.int32, (part, LANES), 0)
            + (me * slim + q * part - kept // 2)
        ).astype(F32)
        c_re, c_im = cos_sin_pi(
            (across * across) * (total / (width * width)) * dist_ref[0]
        )
        c_im = -c_im

        def screen(n, carry):
            at = pl.ds(pl.multiple_of(n * LANES, LANES), LANES)
            for k in range(groups):
                top = slice(k * part, (k + 1) * part)
                low = slice(half + k * part, half + (k + 1) * part)
                s_re = prod[0, top, at] - prod[1, low, at]
                s_im = prod[1, top, at] + prod[0, low, at]
                r_re = rowf[0, k : k + 1, at]
                r_im = rowf[1, k : k + 1, at]
                h_re = r_re * c_re - r_im * c_im
                h_im = r_re * c_im + r_im * c_re
                if conj:
                    h_im = -h_im
                packed[top, at] = (s_re * h_re - s_im * h_im).astype(BF16)
                packed[low, at] = (s_re * h_im + s_im * h_re).astype(BF16)
            return carry

        lax.fori_loop(0, lane_chunks, screen, 0)
        prod[0] = jnp.dot(packed[...], blk_ref[0], preferred_element_type=F32)
        prod[1] = jnp.dot(packed[...], blk_ref[1], preferred_element_type=F32)

        def unmix(n, carry):
            at = pl.ds(pl.multiple_of(n * LANES, LANES), LANES)
            values = []
            for k in range(groups):
                top = slice(k * part, (k + 1) * part)
                low = slice(half + k * part, half + (k + 1) * part)
                u_re = prod[0, top, at] + prod[1, low, at]
                u_im = prod[0, low, at] - prod[1, top, at]
                t_re = twist_ref[0, k : k + 1, at]
                t_im = twist_ref[1, k : k + 1, at]
                values.append(
                    (
                        (u_re * t_re + u_im * t_im).astype(BF16).astype(F32),
                        (u_im * t_re - u_re * t_im).astype(BF16).astype(F32),
                    )
                )
            for p, (re, im) in enumerate(small_dft(values, 1)):
                both = jnp.concatenate([re, im], 0) * (1.0 / total)
                send[slot_out, p, :, at] = both.astype(BF16)
            return carry

        lax.fori_loop(0, lane_chunks, unmix, 0)
        exchange(slot_out)

    def gather_part(slot, q, top):
        near = recv[slot].reshape(span, height)
        return jnp.dot(
            back_ref[pl.ds(top, BLK), q * span : (q + 1) * span],
            near,
            preferred_element_type=F32,
        )

    def spread(first, finish):
        for q in range(chunks - 1):
            arrive(first + q)

            def add(n, carry):
                top = pl.multiple_of(n * BLK, BLK)
                value = gather_part(first + q, q, top)
                at = pl.ds(top, BLK)
                acc[at, :] = value if q == 0 else acc[at, :] + value
                return carry

            lax.fori_loop(0, 2 * col_blocks, add, 0)
        q = chunks - 1
        arrive(first + q)

        def last(n, carry):
            top = pl.multiple_of(n * BLK, BLK)
            low = pl.multiple_of(width + n * BLK, BLK)
            re = gather_part(first + q, q, top)
            im = gather_part(first + q, q, low)
            if chunks > 1:
                re = re + acc[pl.ds(top, BLK), :]
                im = im + acc[pl.ds(low, BLK), :]
            finish(top, low, re * (1.0 / width), im * (1.0 / width))
            return carry

        lax.fori_loop(0, col_blocks, last, 0)

    def weigh(top, low, re, im):
        residual = re * re + im * im - target_t[pl.ds(top, BLK), :]
        field[pl.ds(top, BLK), :] = (residual * re).astype(BF16)
        field[pl.ds(low, BLK), :] = (residual * im).astype(BF16)

    share = width // trials
    per = BLK // share if share < BLK else 1

    def slope(top, low, re, im):
        value = 2.0 * (lens[pl.ds(top, BLK), :] * im - lens[pl.ds(low, BLK), :] * re)
        value = value.astype(BF16)
        if share >= BLK:
            gsend[top // share, pl.ds(pl.multiple_of(top % share, BLK), BLK), :] = value
        else:
            for n in range(per):
                gsend[top // share + n] = value[n * share : (n + 1) * share]

    for q in range(chunks):
        columns(q, q)
        if q == 0:
            pl.semaphore_wait(barrier, groups + trials - 2)
        exchange(q)

    index_k = lax.broadcasted_iota(jnp.int32, (groups, height), 0)
    index_m = lax.broadcasted_iota(jnp.int32, (groups, height), 1)
    freq = index_k + groups * index_m
    signed = jnp.where(freq >= total // 2, freq - total, freq).astype(F32)
    r_cos, r_sin = cos_sin_pi((signed * signed) * (1.0 / total) * dist_ref[0])
    rowf[0] = r_cos
    rowf[1] = -r_sin

    def flip(b, carry):
        rows = pl.ds(pl.multiple_of((b % row_blocks) * BLK, BLK), BLK)
        cols = pl.ds(pl.multiple_of((b // row_blocks) * BLK, BLK), BLK)
        target_t[cols, rows] = target_ref[rows, cols].T
        return carry

    lax.fori_loop(0, row_blocks * col_blocks, flip, 0)

    for q in range(chunks):
        middle(q, chunks + q, q, False)
    spread(chunks, weigh)
    for q in range(chunks):
        columns(2 * chunks + q, q)
        exchange(2 * chunks + q)
    for q in range(chunks):
        middle(2 * chunks + q, 3 * chunks + q, q, True)
    spread(3 * chunks, slope)

    def hand_on(r):
        to = lax.rem(mine + r, trials)
        return pltpu.make_async_remote_copy(
            src_ref=gsend.at[to],
            dst_ref=grecv.at[r],
            send_sem=gsend_sem.at[r],
            recv_sem=grecv_sem.at[r],
            device_id=(to, me),
            device_id_type=MESH,
        )

    for r in range(1, trials):
        hand_on(r).start()
    sum_all = gsend[mine].astype(F32)
    for r in range(1, trials):
        hand_on(r).wait_recv()
        sum_all = sum_all + grecv[r].astype(F32)
    out_ref[...] = sum_all

    for slot in range(4 * chunks):
        for r in range(1, groups):
            copy_to(slot, r).wait_send()
    for r in range(1, trials):
        hand_on(r).wait_send()


def local(phase_map, target, distance, etch_class, class_offset, aperture_start, aperture_stop):
    height, width = phase_map.shape
    kept = width // 2
    groups = lax.axis_size("row")
    trials = lax.axis_size("trial")
    slim = kept // groups
    chunks = 2 if slim % 16 == 0 and slim >= 32 else 1
    side = 2 * slim // chunks
    half = kept // chunks
    share = width // trials
    forward, backward, blk, twist = tables(height, width, kept, groups, chunks)
    import functools

    smem = pl.BlockSpec(memory_space=pltpu.SMEM)
    vmem = pl.BlockSpec(memory_space=pltpu.VMEM)
    out = pl.pallas_call(
        functools.partial(kernel, (groups, trials, height, width, kept, chunks)),
        out_shape=jax.ShapeDtypeStruct((share, height), F32),
        in_specs=[smem] * 5 + [vmem] * 6,
        out_specs=vmem,
        scratch_shapes=[
            pltpu.VMEM((2 * width, height), F32),
            pltpu.VMEM((2 * width, height), BF16),
            pltpu.VMEM((width, height), F32),
            pltpu.VMEM((2, groups, height), F32),
            pltpu.VMEM((2 * width, height), F32),
            pltpu.VMEM((2 * half, height), BF16),
            pltpu.VMEM((2, 2 * half, height), F32),
            pltpu.VMEM((4 * chunks, groups, side, height), BF16),
            pltpu.VMEM((4 * chunks, groups, side, height), BF16),
            pltpu.VMEM((trials, share, height), BF16),
            pltpu.VMEM((trials, share, height), BF16),
            pltpu.SemaphoreType.DMA((4 * chunks, groups)),
            pltpu.SemaphoreType.DMA((4 * chunks, groups)),
            pltpu.SemaphoreType.DMA((trials,)),
            pltpu.SemaphoreType.DMA((trials,)),
        ],
        compiler_params=pltpu.CompilerParams(
            collective_id=0, has_side_effects=True, vmem_limit_bytes=48 * 1024 * 1024
        ),
    )(
        distance,
        etch_class,
        class_offset,
        aperture_start,
        aperture_stop,
        phase_map,
        target,
        forward,
        backward,
        blk,
        twist,
    )
    return out.T


def solution(mesh):
    return jax.shard_map(
        local,
        mesh=mesh,
        in_specs=(
            P("row", None),
            P("row", None),
            P("trial"),
            P("trial", "row", None),
            P(),
            P(),
            P(),
        ),
        out_specs=P("row", "trial"),
        check_vma=False,
    )
```

```python
import functools
import math

import jax
import jax.numpy as jnp
import numpy as np
from jax import lax
from jax.experimental import pallas as pl
from jax.experimental.pallas import tpu as pltpu
from jax.sharding import PartitionSpec as P

BLK = 128
LANES = 128
F32 = jnp.float32
BF16 = jnp.bfloat16
MESH = pl.DeviceIdType.MESH
MAGIC = 12582912.0


def even_fit(func, degree):
    cheb = np.polynomial.chebyshev.Chebyshev.interpolate(func, degree, domain=[0.0, 0.25])
    return [float(c) for c in cheb.convert(kind=np.polynomial.Polynomial).coef]


COS_FIT = even_fit(lambda z: np.cos(np.pi * np.sqrt(z)), 6)
SIN_FIT = even_fit(lambda z: np.pi * np.sinc(np.sqrt(z)), 5)


def horner(coefs, z):
    total = jnp.full_like(z, coefs[-1])
    for c in coefs[-2::-1]:
        total = total * z + c
    return total


def nearest(u):
    return (u + MAGIC) - MAGIC


def turn(u):
    whole = nearest(u)
    rest = u - whole
    z = rest * rest
    return horner(COS_FIT, z), rest * horner(SIN_FIT, z), whole


def cos_sin_pi(u):
    cos, sin, whole = turn(u)
    half = whole * 0.5
    odd = half - nearest(half)
    sign = 1.0 - 8.0 * (odd * odd)
    return cos * sign, sin * sign


def scale_turn(re, im, k, n, sign):
    if k == 0:
        return re, im
    if 4 * k == n:
        return (-im, re) if sign > 0 else (im, -re)
    c = math.cos(2 * math.pi * k / n)
    s = sign * math.sin(2 * math.pi * k / n)
    if 8 * k == n:
        return ((re - im) * c, (re + im) * c) if sign > 0 else ((re + im) * c, (im - re) * c)
    return re * c - im * s, re * s + im * c


def small_dft(values, sign):
    n = len(values)
    if n == 1:
        return values
    even = small_dft(values[0::2], sign)
    odd = small_dft(values[1::2], sign)
    low, high = [], []
    for k in range(n // 2):
        re, im = scale_turn(*odd[k], k, n, sign)
        low.append((even[k][0] + re, even[k][1] + im))
        high.append((even[k][0] - re, even[k][1] - im))
    return low + high


def tables(height, width, kept, groups, chunks):
    slim = kept // groups
    part = slim // chunks
    cols = np.arange(width)
    freqs = np.arange(kept) - kept // 2
    angle = -2.0 * np.pi / width * np.mod(cols[:, None] * freqs[None, :], width)
    re = np.cos(angle).T.reshape(groups, chunks, part, width)
    im = np.sin(angle).T.reshape(groups, chunks, part, width)
    rows_re = np.concatenate([re, -im], 3)
    rows_im = np.concatenate([im, re], 3)
    forward = np.stack([rows_re, rows_im], 2)
    forward = forward.transpose(1, 0, 2, 3, 4).reshape(2 * kept, 2 * width)
    places = np.arange(height)
    angle = -2.0 * np.pi / height * np.mod(places[:, None] * places[None, :], height)
    blk = np.stack([np.cos(angle), np.sin(angle)])
    total = height * groups
    angle = -2.0 * np.pi / total * np.mod(np.arange(groups)[:, None] * places[None, :], total)
    twist = np.stack([np.cos(angle), np.sin(angle)])
    as_bf16 = lambda a: jnp.asarray(a.astype(np.float32).astype(BF16))
    return as_bf16(forward), as_bf16(forward.T), as_bf16(blk), jnp.asarray(twist.astype(np.float32))


def kernel(
    dims,
    dist_ref,
    class_ref,
    level_ref,
    start_ref,
    stop_ref,
    phase_hbm,
    target_hbm,
    fwd_hbm,
    back_hbm,
    blk_hbm,
    twist_hbm,
    out_ref,
    phase_ref,
    target_ref,
    fwd_ref,
    back_ref,
    blk_ref,
    twist_ref,
    fetch_sem,
    lens,
    field,
    target_t,
    rowf,
    acc,
    packed,
    prod,
    send,
    recv,
    gsend,
    grecv,
    send_sem,
    recv_sem,
    gsend_sem,
    grecv_sem,
):
    groups, trials, height, width, kept, chunks = dims
    slim = kept // groups
    part = slim // chunks
    side = 2 * part
    half = groups * part
    span = 2 * kept // chunks
    total = height * groups
    me = lax.axis_index("row")
    mine = lax.axis_index("trial")
    lane_chunks = height // LANES

    fetches = {}

    def fetch(name, source, dest, pieces):
        rows = source.shape[0] // pieces
        made = []
        for n in range(pieces):
            at = pl.ds(n * rows, rows)
            place = sum(len(c) for c in fetches.values()) + n
            made.append(
                pltpu.make_async_copy(source.at[at], dest.at[at], fetch_sem.at[place])
            )
            made[-1].start()
        fetches[name] = made

    def fetched(name):
        for made in fetches[name]:
            made.wait()

    fetch("phase", phase_hbm, phase_ref, height // BLK)
    fetch("fwd", fwd_hbm, fwd_ref, 4)
    fetch("twist", twist_hbm, twist_ref, 1)
    fetch("target", target_hbm, target_ref, 4)
    fetch("blk", blk_hbm, blk_ref, 2)
    fetch("back", back_hbm, back_ref, 4)

    barrier = pltpu.get_barrier_semaphore()
    for r in range(1, groups):
        pl.semaphore_signal(
            barrier, inc=1, device_id=(mine, lax.rem(me + r, groups)), device_id_type=MESH
        )
    for r in range(1, trials):
        pl.semaphore_signal(
            barrier, inc=1, device_id=(lax.rem(mine + r, trials), me), device_id_type=MESH
        )

    row_blocks = height // BLK
    col_blocks = width // BLK

    def lens_block(rb, cb, carry):
        rows = pl.ds(rb * BLK, BLK)
        cols = pl.ds(pl.multiple_of(cb * BLK, BLK), BLK)
        offset = level_ref[class_ref[0, rb, cb]]
        where = me * row_blocks + rb
        inside = jnp.where(
            jnp.logical_and(where >= start_ref[cb], where < stop_ref[cb]), 1.0, 0.0
        ).astype(F32)
        angle = phase_ref[rows, cols].T + offset
        cos, sin, whole = turn(angle * (1.0 / math.pi))
        sign = inside - (2.0 * inside) * (whole * whole)
        re = cos * sign
        im = sin * sign
        low = pl.ds(pl.multiple_of(width + cb * BLK, BLK), BLK)
        lens[cols, rows] = re
        lens[low, rows] = im
        field[cols, rows] = re.astype(BF16)
        field[low, rows] = im.astype(BF16)
        return carry

    for rb in range(row_blocks):
        fetches["phase"][rb].wait()
        lax.fori_loop(0, col_blocks, functools.partial(lens_block, rb), 0)

    def copy_to(slot, r):
        to = lax.rem(me + r, groups)
        return pltpu.make_async_remote_copy(
            src_ref=send.at[slot, to],
            dst_ref=recv.at[slot, me],
            send_sem=send_sem.at[slot, r],
            recv_sem=recv_sem.at[slot, r],
            device_id=(mine, to),
            device_id_type=MESH,
        )

    def exchange(slot):
        for r in range(1, groups):
            copy_to(slot, r).start()
        recv[slot, me] = send[slot, me]

    def arrive(slot):
        for r in range(1, groups):
            copy_to(slot, r).wait_recv()

    def columns(slot, q):
        made = jnp.dot(
            fwd_ref[q * span : (q + 1) * span, :], field[...], preferred_element_type=F32
        )
        send[slot] = made.astype(BF16).reshape(groups, side, height)

    def middle(slot_in, slot_out, q, conj):
        arrive(slot_in)

        def mix(n, carry):
            at = pl.ds(pl.multiple_of(n * LANES, LANES), LANES)
            values = []
            for p in range(groups):
                both = recv[slot_in, p, :, at].astype(F32)
                values.append((both[:part], both[part:]))
            for k, (re, im) in enumerate(small_dft(values, -1)):
                t_re = twist_ref[0, k : k + 1, at]
                t_im = twist_ref[1, k : k + 1, at]
                packed[k * part : (k + 1) * part, at] = (re * t_re - im * t_im).astype(BF16)
                packed[half + k * part : half + (k + 1) * part, at] = (
                    re * t_im + im * t_re
                ).astype(BF16)
            return carry

        lax.fori_loop(0, lane_chunks, mix, 0)
        prod[0] = jnp.dot(packed[...], blk_ref[0], preferred_element_type=F32)
        prod[1] = jnp.dot(packed[...], blk_ref[1], preferred_element_type=F32)
        across = (
            lax.broadcasted_iota(jnp.int32, (part, LANES), 0)
            + (me * slim + q * part - kept // 2)
        ).astype(F32)
        c_re, c_im = cos_sin_pi(
            (across * across) * (total / (width * width)) * dist_ref[0]
        )
        c_im = -c_im

        def screen(n, carry):
            at = pl.ds(pl.multiple_of(n * LANES, LANES), LANES)
            for k in range(groups):
                top = slice(k * part, (k + 1) * part)
                low = slice(half + k * part, half + (k + 1) * part)
                s_re = prod[0, top, at] - prod[1, low, at]
                s_im = prod[1, top, at] + prod[0, low, at]
                r_re = rowf[0, k : k + 1, at]
                r_im = rowf[1, k : k + 1, at]
                h_re = r_re * c_re - r_im * c_im
                h_im = r_re * c_im + r_im * c_re
                if conj:
                    h_im = -h_im
                packed[top, at] = (s_re * h_re - s_im * h_im).astype(BF16)
                packed[low, at] = (s_re * h_im + s_im * h_re).astype(BF16)
            return carry

        lax.fori_loop(0, lane_chunks, screen, 0)
        prod[0] = jnp.dot(packed[...], blk_ref[0], preferred_element_type=F32)
        prod[1] = jnp.dot(packed[...], blk_ref[1], preferred_element_type=F32)

        def unmix(n, carry):
            at = pl.ds(pl.multiple_of(n * LANES, LANES), LANES)
            values = []
            for k in range(groups):
                top = slice(k * part, (k + 1) * part)
                low = slice(half + k * part, half + (k + 1) * part)
                u_re = prod[0, top, at] + prod[1, low, at]
                u_im = prod[0, low, at] - prod[1, top, at]
                t_re = twist_ref[0, k : k + 1, at]
                t_im = twist_ref[1, k : k + 1, at]
                values.append(
                    (
                        (u_re * t_re + u_im * t_im).astype(BF16).astype(F32),
                        (u_im * t_re - u_re * t_im).astype(BF16).astype(F32),
                    )
                )
            for p, (re, im) in enumerate(small_dft(values, 1)):
                both = jnp.concatenate([re, im], 0) * (1.0 / total)
                send[slot_out, p, :, at] = both.astype(BF16)
            return carry

        lax.fori_loop(0, lane_chunks, unmix, 0)
        exchange(slot_out)

    def gather_part(slot, q, top, block=BLK):
        near = recv[slot].reshape(span, height)
        return jnp.dot(
            back_ref[pl.ds(top, block), q * span : (q + 1) * span],
            near,
            preferred_element_type=F32,
        )

    def spread(first, block, finish):
        for q in range(chunks - 1):
            arrive(first + q)

            def add(n, carry):
                top = pl.multiple_of(n * BLK, BLK)
                value = gather_part(first + q, q, top)
                at = pl.ds(top, BLK)
                acc[at, :] = value if q == 0 else acc[at, :] + value
                return carry

            lax.fori_loop(0, 2 * col_blocks, add, 0)
        q = chunks - 1
        arrive(first + q)

        for n in range(width // block):
            finish(n, functools.partial(result, first + q, q, block))

    def result(slot, q, block, n):
        top = pl.multiple_of(n * block, block)
        low = pl.multiple_of(width + n * block, block)
        re = gather_part(slot, q, top, block)
        im = gather_part(slot, q, low, block)
        if chunks > 1:
            re = re + acc[pl.ds(top, block), :]
            im = im + acc[pl.ds(low, block), :]
        return pl.ds(top, block), pl.ds(low, block), re * (1.0 / width), im * (1.0 / width)

    def weigh(n, made):
        top, low, re, im = made(n)
        residual = re * re + im * im - target_t[top, :]
        field[top, :] = (residual * re).astype(BF16)
        field[low, :] = (residual * im).astype(BF16)

    share = width // trials

    def hand_on(r):
        to = lax.rem(mine + r, trials)
        return pltpu.make_async_remote_copy(
            src_ref=gsend.at[to],
            dst_ref=grecv.at[r],
            send_sem=gsend_sem.at[r],
            recv_sem=grecv_sem.at[r],
            device_id=(to, me),
            device_id_type=MESH,
        )

    def slope(n, made):
        r = (n + 1) % trials
        to = lax.rem(mine + r, trials)
        top, low, re, im = made(to)
        value = 2.0 * (lens[top, :] * im - lens[low, :] * re)
        gsend[to] = value.astype(BF16)
        if r:
            hand_on(r).start()

    fetched("fwd")
    for q in range(chunks):
        columns(q, q)
        if q == 0:
            pl.semaphore_wait(barrier, groups + trials - 2)
        exchange(q)

    index_k = lax.broadcasted_iota(jnp.int32, (groups, height), 0)
    index_m = lax.broadcasted_iota(jnp.int32, (groups, height), 1)
    freq = index_k + groups * index_m
    signed = jnp.where(freq >= total // 2, freq - total, freq).astype(F32)
    r_cos, r_sin = cos_sin_pi((signed * signed) * (1.0 / total) * dist_ref[0])
    rowf[0] = r_cos
    rowf[1] = -r_sin

    def flip(b, carry):
        rows = pl.ds(pl.multiple_of((b % row_blocks) * BLK, BLK), BLK)
        cols = pl.ds(pl.multiple_of((b // row_blocks) * BLK, BLK), BLK)
        target_t[cols, rows] = target_ref[rows, cols].T
        return carry

    fetched("target")
    lax.fori_loop(0, row_blocks * col_blocks, flip, 0)
    fetched("twist")
    fetched("blk")

    for q in range(chunks):
        middle(q, chunks + q, q, False)
        if q == 0:
            fetched("back")
    spread(chunks, BLK, weigh)
    for q in range(chunks):
        columns(2 * chunks + q, q)
        exchange(2 * chunks + q)
    for q in range(chunks):
        middle(2 * chunks + q, 3 * chunks + q, q, True)
    spread(3 * chunks, share, slope)

    sum_all = gsend[mine].astype(F32)
    for r in range(1, trials):
        hand_on(r).wait_recv()
        sum_all = sum_all + grecv[r].astype(F32)
    out_ref[...] = sum_all

    for slot in range(4 * chunks):
        for r in range(1, groups):
            copy_to(slot, r).wait_send()
    for r in range(1, trials):
        hand_on(r).wait_send()


def local(phase_map, target, distance, etch_class, class_offset, aperture_start, aperture_stop):
    height, width = phase_map.shape
    kept = width // 2
    groups = lax.axis_size("row")
    trials = lax.axis_size("trial")
    slim = kept // groups
    chunks = 2 if slim % 16 == 0 and slim >= 32 else 1
    side = 2 * slim // chunks
    half = kept // chunks
    share = width // trials
    forward, backward, blk, twist = tables(height, width, kept, groups, chunks)
    smem = pl.BlockSpec(memory_space=pltpu.SMEM)
    hbm = pl.BlockSpec(memory_space=pltpu.HBM)
    vmem = pl.BlockSpec(memory_space=pltpu.VMEM)
    out = pl.pallas_call(
        functools.partial(kernel, (groups, trials, height, width, kept, chunks)),
        out_shape=jax.ShapeDtypeStruct((share, height), F32),
        in_specs=[smem] * 5 + [hbm] * 6,
        out_specs=vmem,
        scratch_shapes=[
            pltpu.VMEM(phase_map.shape, F32),
            pltpu.VMEM(target.shape, F32),
            pltpu.VMEM(forward.shape, BF16),
            pltpu.VMEM(backward.shape, BF16),
            pltpu.VMEM(blk.shape, BF16),
            pltpu.VMEM(twist.shape, F32),
            pltpu.SemaphoreType.DMA((height // BLK + 15,)),
            pltpu.VMEM((2 * width, height), F32),
            pltpu.VMEM((2 * width, height), BF16),
            pltpu.VMEM((width, height), F32),
            pltpu.VMEM((2, groups, height), F32),
            pltpu.VMEM((2 * width, height), F32),
            pltpu.VMEM((2 * half, height), BF16),
            pltpu.VMEM((2, 2 * half, height), F32),
            pltpu.VMEM((4 * chunks, groups, side, height), BF16),
            pltpu.VMEM((4 * chunks, groups, side, height), BF16),
            pltpu.VMEM((trials, share, height), BF16),
            pltpu.VMEM((trials, share, height), BF16),
            pltpu.SemaphoreType.DMA((4 * chunks, groups)),
            pltpu.SemaphoreType.DMA((4 * chunks, groups)),
            pltpu.SemaphoreType.DMA((trials,)),
            pltpu.SemaphoreType.DMA((trials,)),
        ],
        compiler_params=pltpu.CompilerParams(
            collective_id=0, has_side_effects=True, vmem_limit_bytes=48 * 1024 * 1024
        ),
    )(
        distance,
        etch_class,
        class_offset,
        aperture_start,
        aperture_stop,
        phase_map,
        target,
        forward,
        backward,
        blk,
        twist,
    )
    return out.T


def solution(mesh):
    return jax.shard_map(
        local,
        mesh=mesh,
        in_specs=(
            P("row", None),
            P("row", None),
            P("trial"),
            P("trial", "row", None),
            P(),
            P(),
            P(),
        ),
        out_specs=P("row", "trial"),
        check_vma=False,
    )
```

```python
import functools
import math

import jax
import jax.numpy as jnp
import numpy as np
from jax import lax
from jax.experimental import pallas as pl
from jax.experimental.pallas import tpu as pltpu
from jax.sharding import PartitionSpec as P

BLK = 128
LANES = 128
F32 = jnp.float32
BF16 = jnp.bfloat16
MESH = pl.DeviceIdType.MESH
MAGIC = 12582912.0


def even_fit(func, degree):
    cheb = np.polynomial.chebyshev.Chebyshev.interpolate(func, degree, domain=[0.0, 0.25])
    return [float(c) for c in cheb.convert(kind=np.polynomial.Polynomial).coef]


COS_FIT = even_fit(lambda z: np.cos(np.pi * np.sqrt(z)), 6)
SIN_FIT = even_fit(lambda z: np.pi * np.sinc(np.sqrt(z)), 5)


def horner(coefs, z):
    total = jnp.full_like(z, coefs[-1])
    for c in coefs[-2::-1]:
        total = total * z + c
    return total


def nearest(u):
    return (u + MAGIC) - MAGIC


def turn(u):
    whole = nearest(u)
    rest = u - whole
    z = rest * rest
    return horner(COS_FIT, z), rest * horner(SIN_FIT, z), whole


def cos_sin_pi(u):
    cos, sin, whole = turn(u)
    half = whole * 0.5
    odd = half - nearest(half)
    sign = 1.0 - 8.0 * (odd * odd)
    return cos * sign, sin * sign


def scale_turn(re, im, k, n, sign):
    if k == 0:
        return re, im
    if 4 * k == n:
        return (-im, re) if sign > 0 else (im, -re)
    c = math.cos(2 * math.pi * k / n)
    s = sign * math.sin(2 * math.pi * k / n)
    if 8 * k == n:
        return ((re - im) * c, (re + im) * c) if sign > 0 else ((re + im) * c, (im - re) * c)
    return re * c - im * s, re * s + im * c


def small_dft(values, sign):
    n = len(values)
    if n == 1:
        return values
    even = small_dft(values[0::2], sign)
    odd = small_dft(values[1::2], sign)
    low, high = [], []
    for k in range(n // 2):
        re, im = scale_turn(*odd[k], k, n, sign)
        low.append((even[k][0] + re, even[k][1] + im))
        high.append((even[k][0] - re, even[k][1] - im))
    return low + high


def tables(height, width, kept, groups, chunks):
    slim = kept // groups
    part = slim // chunks
    cols = np.arange(width)
    freqs = np.arange(kept) - kept // 2
    angle = -2.0 * np.pi / width * np.mod(cols[:, None] * freqs[None, :], width)
    re = np.cos(angle).T.reshape(groups, chunks, part, width)
    im = np.sin(angle).T.reshape(groups, chunks, part, width)
    rows_re = np.concatenate([re, -im], 3)
    rows_im = np.concatenate([im, re], 3)
    forward = np.stack([rows_re, rows_im], 2)
    forward = forward.transpose(1, 0, 2, 3, 4).reshape(2 * kept, 2 * width)
    places = np.arange(height)
    angle = -2.0 * np.pi / height * np.mod(places[:, None] * places[None, :], height)
    blk = np.stack([np.cos(angle), np.sin(angle)])
    total = height * groups
    angle = -2.0 * np.pi / total * np.mod(np.arange(groups)[:, None] * places[None, :], total)
    twist = np.stack([np.cos(angle), np.sin(angle)])
    as_bf16 = lambda a: jnp.asarray(a.astype(np.float32).astype(BF16))
    return as_bf16(forward), as_bf16(forward.T), as_bf16(blk), jnp.asarray(twist.astype(np.float32))


def kernel(
    dims,
    dist_ref,
    class_ref,
    level_ref,
    start_ref,
    stop_ref,
    phase_hbm,
    target_hbm,
    fwd_hbm,
    back_hbm,
    blk_hbm,
    twist_hbm,
    out_ref,
    phase_ref,
    target_ref,
    fwd_ref,
    back_ref,
    blk_ref,
    twist_ref,
    fetch_sem,
    lens,
    field,
    target_t,
    rowf,
    acc,
    packed,
    prod,
    send,
    recv,
    gsend,
    grecv,
    send_sem,
    recv_sem,
    gsend_sem,
    grecv_sem,
):
    groups, trials, height, width, kept, chunks = dims
    slim = kept // groups
    part = slim // chunks
    side = 2 * part
    half = groups * part
    span = 2 * kept // chunks
    total = height * groups
    me = lax.axis_index("row")
    mine = lax.axis_index("trial")
    lane_chunks = height // LANES

    fetches = {}

    def fetch(name, source, dest, pieces):
        rows = source.shape[0] // pieces
        made = []
        for n in range(pieces):
            at = pl.ds(n * rows, rows)
            place = sum(len(c) for c in fetches.values()) + n
            made.append(
                pltpu.make_async_copy(source.at[at], dest.at[at], fetch_sem.at[place])
            )
            made[-1].start()
        fetches[name] = made

    def fetched(name):
        for made in fetches[name]:
            made.wait()

    fetch("phase", phase_hbm, phase_ref, height // BLK)
    fetch("fwd", fwd_hbm, fwd_ref, 4)
    fetch("twist", twist_hbm, twist_ref, 1)
    fetch("target", target_hbm, target_ref, 4)
    fetch("blk", blk_hbm, blk_ref, 2)
    fetch("back", back_hbm, back_ref, 4)

    barrier = pltpu.get_barrier_semaphore()
    for r in range(1, groups):
        pl.semaphore_signal(
            barrier, inc=1, device_id=(mine, lax.rem(me + r, groups)), device_id_type=MESH
        )
    for r in range(1, trials):
        pl.semaphore_signal(
            barrier, inc=1, device_id=(lax.rem(mine + r, trials), me), device_id_type=MESH
        )

    row_blocks = height // BLK
    col_blocks = width // BLK

    def lens_block(rb, cb, carry):
        rows = pl.ds(rb * BLK, BLK)
        cols = pl.ds(pl.multiple_of(cb * BLK, BLK), BLK)
        offset = level_ref[class_ref[0, rb, cb]]
        where = me * row_blocks + rb
        inside = jnp.where(
            jnp.logical_and(where >= start_ref[cb], where < stop_ref[cb]), 1.0, 0.0
        ).astype(F32)
        angle = phase_ref[rows, cols].T + offset
        cos, sin, whole = turn(angle * (1.0 / math.pi))
        sign = inside - (2.0 * inside) * (whole * whole)
        re = cos * sign
        im = sin * sign
        low = pl.ds(pl.multiple_of(width + cb * BLK, BLK), BLK)
        lens[cols, rows] = re
        lens[low, rows] = im
        field[cols, rows] = re.astype(BF16)
        field[low, rows] = im.astype(BF16)
        return carry

    for rb in range(row_blocks):
        fetches["phase"][rb].wait()
        lax.fori_loop(0, col_blocks, functools.partial(lens_block, rb), 0)

    def copy_to(slot, r):
        to = lax.rem(me + r, groups)
        return pltpu.make_async_remote_copy(
            src_ref=send.at[slot, to],
            dst_ref=recv.at[slot, me],
            send_sem=send_sem.at[slot, r],
            recv_sem=recv_sem.at[slot, r],
            device_id=(mine, to),
            device_id_type=MESH,
        )

    def exchange(slot):
        for r in range(1, groups):
            copy_to(slot, r).start()
        recv[slot, me] = send[slot, me]

    def arrive(slot):
        for r in range(1, groups):
            copy_to(slot, r).wait_recv()

    def columns(slot, q):
        made = jnp.dot(
            fwd_ref[q * span : (q + 1) * span, :], field[...], preferred_element_type=F32
        )
        send[slot] = made.astype(BF16).reshape(groups, side, height)

    def middle(slot_in, slot_out, q, conj):
        arrive(slot_in)

        def mix(n, carry):
            at = pl.ds(pl.multiple_of(n * LANES, LANES), LANES)
            values = []
            for p in range(groups):
                both = recv[slot_in, p, :, at].astype(F32)
                values.append((both[:part], both[part:]))
            for k, (re, im) in enumerate(small_dft(values, -1)):
                t_re = twist_ref[0, k : k + 1, at]
                t_im = twist_ref[1, k : k + 1, at]
                packed[k * part : (k + 1) * part, at] = (re * t_re - im * t_im).astype(BF16)
                packed[half + k * part : half + (k + 1) * part, at] = (
                    re * t_im + im * t_re
                ).astype(BF16)
            return carry

        lax.fori_loop(0, lane_chunks, mix, 0)
        prod[0] = jnp.dot(packed[...], blk_ref[0], preferred_element_type=F32)
        prod[1] = jnp.dot(packed[...], blk_ref[1], preferred_element_type=F32)
        across = (
            lax.broadcasted_iota(jnp.int32, (part, LANES), 0)
            + (me * slim + q * part - kept // 2)
        ).astype(F32)
        c_re, c_im = cos_sin_pi(
            (across * across) * (total / (width * width)) * dist_ref[0]
        )
        c_im = -c_im

        def screen(n, carry):
            at = pl.ds(pl.multiple_of(n * LANES, LANES), LANES)
            for k in range(groups):
                top = slice(k * part, (k + 1) * part)
                low = slice(half + k * part, half + (k + 1) * part)
                s_re = prod[0, top, at] - prod[1, low, at]
                s_im = prod[1, top, at] + prod[0, low, at]
                r_re = rowf[0, k : k + 1, at]
                r_im = rowf[1, k : k + 1, at]
                h_re = r_re * c_re - r_im * c_im
                h_im = r_re * c_im + r_im * c_re
                if conj:
                    h_im = -h_im
                packed[top, at] = (s_re * h_re - s_im * h_im).astype(BF16)
                packed[low, at] = (s_re * h_im + s_im * h_re).astype(BF16)
            return carry

        lax.fori_loop(0, lane_chunks, screen, 0)
        prod[0] = jnp.dot(packed[...], blk_ref[0], preferred_element_type=F32)
        prod[1] = jnp.dot(packed[...], blk_ref[1], preferred_element_type=F32)

        def unmix(n, carry):
            at = pl.ds(pl.multiple_of(n * LANES, LANES), LANES)
            values = []
            for k in range(groups):
                top = slice(k * part, (k + 1) * part)
                low = slice(half + k * part, half + (k + 1) * part)
                u_re = prod[0, top, at] + prod[1, low, at]
                u_im = prod[0, low, at] - prod[1, top, at]
                t_re = twist_ref[0, k : k + 1, at]
                t_im = twist_ref[1, k : k + 1, at]
                values.append(
                    (
                        (u_re * t_re + u_im * t_im).astype(BF16).astype(F32),
                        (u_im * t_re - u_re * t_im).astype(BF16).astype(F32),
                    )
                )
            for p, (re, im) in enumerate(small_dft(values, 1)):
                both = jnp.concatenate([re, im], 0) * (1.0 / total)
                send[slot_out, p, :, at] = both.astype(BF16)
            return carry

        lax.fori_loop(0, lane_chunks, unmix, 0)
        exchange(slot_out)

    def gather_part(slot, q, top, block=BLK):
        near = recv[slot].reshape(span, height)
        return jnp.dot(
            back_ref[pl.ds(top, block), q * span : (q + 1) * span],
            near,
            preferred_element_type=F32,
        )

    def spread(first, block, finish):
        for q in range(chunks - 1):
            arrive(first + q)

            def add(n, carry):
                top = pl.multiple_of(n * BLK, BLK)
                value = gather_part(first + q, q, top)
                at = pl.ds(top, BLK)
                acc[at, :] = value if q == 0 else acc[at, :] + value
                return carry

            lax.fori_loop(0, 2 * col_blocks, add, 0)
        q = chunks - 1
        arrive(first + q)

        for n in range(width // block):
            finish(n, functools.partial(result, first + q, q, block))

    def result(slot, q, block, n):
        top = pl.multiple_of(n * block, block)
        low = pl.multiple_of(width + n * block, block)
        re = gather_part(slot, q, top, block)
        im = gather_part(slot, q, low, block)
        if chunks > 1:
            re = re + acc[pl.ds(top, block), :]
            im = im + acc[pl.ds(low, block), :]
        return pl.ds(top, block), pl.ds(low, block), re * (1.0 / width), im * (1.0 / width)

    def weigh(n, made):
        top, low, re, im = made(n)
        residual = re * re + im * im - target_t[top, :]
        field[top, :] = (residual * re).astype(BF16)
        field[low, :] = (residual * im).astype(BF16)

    share = width // trials

    def hand_on(r):
        to = lax.rem(mine + r, trials)
        return pltpu.make_async_remote_copy(
            src_ref=gsend.at[to],
            dst_ref=grecv.at[r],
            send_sem=gsend_sem.at[r],
            recv_sem=grecv_sem.at[r],
            device_id=(to, me),
            device_id_type=MESH,
        )

    def slope(n, made):
        r = (n + 1) % trials
        to = lax.rem(mine + r, trials)
        top, low, re, im = made(to)
        value = 2.0 * (lens[top, :] * im - lens[low, :] * re)
        gsend[to] = value.astype(BF16)
        if r:
            hand_on(r).start()

    fetched("fwd")
    for q in range(chunks):
        columns(q, q)
        if q == 0:
            pl.semaphore_wait(barrier, groups + trials - 2)
        exchange(q)

    index_k = lax.broadcasted_iota(jnp.int32, (groups, height), 0)
    index_m = lax.broadcasted_iota(jnp.int32, (groups, height), 1)
    freq = index_k + groups * index_m
    signed = jnp.where(freq >= total // 2, freq - total, freq).astype(F32)
    r_cos, r_sin = cos_sin_pi((signed * signed) * (1.0 / total) * dist_ref[0])
    rowf[0] = r_cos
    rowf[1] = -r_sin

    def flip(b, carry):
        rows = pl.ds(pl.multiple_of((b % row_blocks) * BLK, BLK), BLK)
        cols = pl.ds(pl.multiple_of((b // row_blocks) * BLK, BLK), BLK)
        target_t[cols, rows] = target_ref[rows, cols].T
        return carry

    fetched("target")
    lax.fori_loop(0, row_blocks * col_blocks, flip, 0)
    fetched("twist")
    fetched("blk")

    for q in range(chunks):
        middle(q, chunks + q, q, False)
        if q == 0:
            fetched("back")
    spread(chunks, BLK, weigh)
    for q in range(chunks):
        columns(2 * chunks + q, q)
        exchange(2 * chunks + q)
    for q in range(chunks):
        middle(2 * chunks + q, 3 * chunks + q, q, True)
    spread(3 * chunks, share, slope)

    sum_all = gsend[mine].astype(F32)
    for r in range(1, trials):
        hand_on(r).wait_recv()
        sum_all = sum_all + grecv[r].astype(F32)
    out_ref[...] = sum_all

    for slot in range(4 * chunks):
        for r in range(1, groups):
            copy_to(slot, r).wait_send()
    for r in range(1, trials):
        hand_on(r).wait_send()


def local(phase_map, target, distance, etch_class, class_offset, aperture_start, aperture_stop):
    height, width = phase_map.shape
    kept = width // 2
    groups = lax.axis_size("row")
    trials = lax.axis_size("trial")
    slim = kept // groups
    chunks = 2 if slim % 16 == 0 and slim >= 32 else 1
    side = 2 * slim // chunks
    half = kept // chunks
    share = width // trials
    forward, backward, blk, twist = tables(height, width, kept, groups, chunks)
    smem = pl.BlockSpec(memory_space=pltpu.SMEM)
    hbm = pl.BlockSpec(memory_space=pltpu.HBM)
    vmem = pl.BlockSpec(memory_space=pltpu.VMEM)
    out = pl.pallas_call(
        functools.partial(kernel, (groups, trials, height, width, kept, chunks)),
        out_shape=jax.ShapeDtypeStruct((share, height), F32),
        in_specs=[smem] * 5 + [hbm] * 6,
        out_specs=vmem,
        scratch_shapes=[
            pltpu.VMEM(phase_map.shape, F32),
            pltpu.VMEM(target.shape, F32),
            pltpu.VMEM(forward.shape, BF16),
            pltpu.VMEM(backward.shape, BF16),
            pltpu.VMEM(blk.shape, BF16),
            pltpu.VMEM(twist.shape, F32),
            pltpu.SemaphoreType.DMA((height // BLK + 15,)),
            pltpu.VMEM((2 * width, height), F32),
            pltpu.VMEM((2 * width, height), BF16),
            pltpu.VMEM((width, height), F32),
            pltpu.VMEM((2, groups, height), F32),
            pltpu.VMEM((2 * width, height), F32),
            pltpu.VMEM((2 * half, height), BF16),
            pltpu.VMEM((2, 2 * half, height), F32),
            pltpu.VMEM((4 * chunks, groups, side, height), BF16),
            pltpu.VMEM((4 * chunks, groups, side, height), BF16),
            pltpu.VMEM((trials, share, height), BF16),
            pltpu.VMEM((trials, share, height), BF16),
            pltpu.SemaphoreType.DMA((4 * chunks, groups)),
            pltpu.SemaphoreType.DMA((4 * chunks, groups)),
            pltpu.SemaphoreType.DMA((trials,)),
            pltpu.SemaphoreType.DMA((trials,)),
        ],
        compiler_params=pltpu.CompilerParams(
            collective_id=0, has_side_effects=True, vmem_limit_bytes=67_043_328
        ),
    )(
        distance,
        etch_class,
        class_offset,
        aperture_start,
        aperture_stop,
        phase_map,
        target,
        forward,
        backward,
        blk,
        twist,
    )
    return out.T


def solution(mesh):
    return jax.shard_map(
        local,
        mesh=mesh,
        in_specs=(
            P("row", None),
            P("row", None),
            P("trial"),
            P("trial", "row", None),
            P(),
            P(),
            P(),
        ),
        out_specs=P("row", "trial"),
        check_vma=False,
    )
```

```python
import functools
import math

import jax
import jax.numpy as jnp
import numpy as np
from jax import lax
from jax.experimental import pallas as pl
from jax.experimental.pallas import tpu as pltpu
from jax.sharding import PartitionSpec as P

BLK = 128
LANES = 128
F32 = jnp.float32
BF16 = jnp.bfloat16
MESH = pl.DeviceIdType.MESH
MAGIC = 12582912.0


def even_fit(func, degree):
    cheb = np.polynomial.chebyshev.Chebyshev.interpolate(func, degree, domain=[0.0, 0.25])
    return [float(c) for c in cheb.convert(kind=np.polynomial.Polynomial).coef]


COS_FIT = even_fit(lambda z: np.cos(np.pi * np.sqrt(z)), 6)
SIN_FIT = even_fit(lambda z: np.pi * np.sinc(np.sqrt(z)), 5)


def horner(coefs, z):
    total = jnp.full_like(z, coefs[-1])
    for c in coefs[-2::-1]:
        total = total * z + c
    return total


def nearest(u):
    return (u + MAGIC) - MAGIC


def turn(u):
    whole = nearest(u)
    rest = u - whole
    z = rest * rest
    return horner(COS_FIT, z), rest * horner(SIN_FIT, z), whole


def cos_sin_pi(u):
    cos, sin, whole = turn(u)
    half = whole * 0.5
    odd = half - nearest(half)
    sign = 1.0 - 8.0 * (odd * odd)
    return cos * sign, sin * sign


def scale_turn(re, im, k, n, sign):
    if k == 0:
        return re, im
    if 4 * k == n:
        return (-im, re) if sign > 0 else (im, -re)
    c = math.cos(2 * math.pi * k / n)
    s = sign * math.sin(2 * math.pi * k / n)
    if 8 * k == n:
        return ((re - im) * c, (re + im) * c) if sign > 0 else ((re + im) * c, (im - re) * c)
    return re * c - im * s, re * s + im * c


def small_dft(values, sign):
    n = len(values)
    if n == 1:
        return values
    even = small_dft(values[0::2], sign)
    odd = small_dft(values[1::2], sign)
    low, high = [], []
    for k in range(n // 2):
        re, im = scale_turn(*odd[k], k, n, sign)
        low.append((even[k][0] + re, even[k][1] + im))
        high.append((even[k][0] - re, even[k][1] - im))
    return low + high


def tables(height, width, kept, groups, chunks):
    slim = kept // groups
    part = slim // chunks
    cols = np.arange(width)
    freqs = np.arange(kept) - kept // 2
    angle = -2.0 * np.pi / width * np.mod(cols[:, None] * freqs[None, :], width)
    re = np.cos(angle).T.reshape(groups, chunks, part, width)
    im = np.sin(angle).T.reshape(groups, chunks, part, width)
    rows_re = np.concatenate([re, -im], 3)
    rows_im = np.concatenate([im, re], 3)
    forward = np.stack([rows_re, rows_im], 2)
    forward = forward.transpose(1, 0, 2, 3, 4).reshape(2 * kept, 2 * width)
    places = np.arange(height)
    angle = -2.0 * np.pi / height * np.mod(places[:, None] * places[None, :], height)
    blk = np.stack([np.cos(angle), np.sin(angle)])
    total = height * groups
    angle = -2.0 * np.pi / total * np.mod(np.arange(groups)[:, None] * places[None, :], total)
    twist = np.stack([np.cos(angle), np.sin(angle)])
    as_bf16 = lambda a: jnp.asarray(a.astype(np.float32).astype(BF16))
    return as_bf16(forward), as_bf16(forward.T), as_bf16(blk), jnp.asarray(twist.astype(np.float32))


def kernel(
    dims,
    dist_ref,
    class_ref,
    level_ref,
    start_ref,
    stop_ref,
    phase_hbm,
    target_hbm,
    fwd_hbm,
    back_hbm,
    blk_hbm,
    twist_hbm,
    out_ref,
    phase_ref,
    target_ref,
    fwd_ref,
    back_ref,
    blk_ref,
    twist_ref,
    fetch_sem,
    lens,
    field,
    target_t,
    rowf,
    acc,
    packed,
    prod,
    send,
    recv,
    gsend,
    grecv,
    send_sem,
    recv_sem,
    gsend_sem,
    grecv_sem,
):
    groups, trials, height, width, kept, chunks = dims
    slim = kept // groups
    part = slim // chunks
    side = 2 * part
    half = groups * part
    span = 2 * kept // chunks
    total = height * groups
    me = lax.axis_index("row")
    mine = lax.axis_index("trial")
    lane_chunks = height // LANES

    fetches = {}

    def fetch(name, source, dest, pieces):
        rows = source.shape[0] // pieces
        made = []
        for n in range(pieces):
            at = pl.ds(n * rows, rows)
            place = sum(len(c) for c in fetches.values()) + n
            made.append(
                pltpu.make_async_copy(source.at[at], dest.at[at], fetch_sem.at[place])
            )
            made[-1].start()
        fetches[name] = made

    def fetched(name):
        for made in fetches[name]:
            made.wait()

    fetch("phase", phase_hbm, phase_ref, height // BLK)
    fetch("fwd", fwd_hbm, fwd_ref, 4)

    barrier = pltpu.get_barrier_semaphore()
    for r in range(1, groups):
        pl.semaphore_signal(
            barrier, inc=1, device_id=(mine, lax.rem(me + r, groups)), device_id_type=MESH
        )
    for r in range(1, trials):
        pl.semaphore_signal(
            barrier, inc=1, device_id=(lax.rem(mine + r, trials), me), device_id_type=MESH
        )

    row_blocks = height // BLK
    col_blocks = width // BLK

    def lens_block(rb, cb, carry):
        rows = pl.ds(rb * BLK, BLK)
        cols = pl.ds(pl.multiple_of(cb * BLK, BLK), BLK)
        offset = level_ref[class_ref[0, rb, cb]]
        where = me * row_blocks + rb
        inside = jnp.where(
            jnp.logical_and(where >= start_ref[cb], where < stop_ref[cb]), 1.0, 0.0
        ).astype(F32)
        angle = phase_ref[rows, cols].T + offset
        cos, sin, whole = turn(angle * (1.0 / math.pi))
        sign = inside - (2.0 * inside) * (whole * whole)
        re = cos * sign
        im = sin * sign
        low = pl.ds(pl.multiple_of(width + cb * BLK, BLK), BLK)
        lens[cols, rows] = re
        lens[low, rows] = im
        field[cols, rows] = re.astype(BF16)
        field[low, rows] = im.astype(BF16)
        return carry

    for rb in range(row_blocks):
        fetches["phase"][rb].wait()
        lax.fori_loop(0, col_blocks, functools.partial(lens_block, rb), 0)

    def copy_to(slot, r):
        to = lax.rem(me + r, groups)
        return pltpu.make_async_remote_copy(
            src_ref=send.at[slot, to],
            dst_ref=recv.at[slot, me],
            send_sem=send_sem.at[slot, r],
            recv_sem=recv_sem.at[slot, r],
            device_id=(mine, to),
            device_id_type=MESH,
        )

    def exchange(slot):
        for r in range(1, groups):
            copy_to(slot, r).start()
        recv[slot, me] = send[slot, me]

    def arrive(slot):
        for r in range(1, groups):
            copy_to(slot, r).wait_recv()

    def columns(slot, q):
        made = jnp.dot(
            fwd_ref[q * span : (q + 1) * span, :], field[...], preferred_element_type=F32
        )
        send[slot] = made.astype(BF16).reshape(groups, side, height)

    def middle(slot_in, slot_out, q, conj):
        arrive(slot_in)

        def mix(n, carry):
            at = pl.ds(pl.multiple_of(n * LANES, LANES), LANES)
            values = []
            for p in range(groups):
                both = recv[slot_in, p, :, at].astype(F32)
                values.append((both[:part], both[part:]))
            for k, (re, im) in enumerate(small_dft(values, -1)):
                t_re = twist_ref[0, k : k + 1, at]
                t_im = twist_ref[1, k : k + 1, at]
                packed[k * part : (k + 1) * part, at] = (re * t_re - im * t_im).astype(BF16)
                packed[half + k * part : half + (k + 1) * part, at] = (
                    re * t_im + im * t_re
                ).astype(BF16)
            return carry

        lax.fori_loop(0, lane_chunks, mix, 0)
        prod[0] = jnp.dot(packed[...], blk_ref[0], preferred_element_type=F32)
        prod[1] = jnp.dot(packed[...], blk_ref[1], preferred_element_type=F32)
        across = (
            lax.broadcasted_iota(jnp.int32, (part, LANES), 0)
            + (me * slim + q * part - kept // 2)
        ).astype(F32)
        c_re, c_im = cos_sin_pi(
            (across * across) * (total / (width * width)) * dist_ref[0]
        )
        c_im = -c_im

        def screen(n, carry):
            at = pl.ds(pl.multiple_of(n * LANES, LANES), LANES)
            for k in range(groups):
                top = slice(k * part, (k + 1) * part)
                low = slice(half + k * part, half + (k + 1) * part)
                s_re = prod[0, top, at] - prod[1, low, at]
                s_im = prod[1, top, at] + prod[0, low, at]
                r_re = rowf[0, k : k + 1, at]
                r_im = rowf[1, k : k + 1, at]
                h_re = r_re * c_re - r_im * c_im
                h_im = r_re * c_im + r_im * c_re
                if conj:
                    h_im = -h_im
                packed[top, at] = (s_re * h_re - s_im * h_im).astype(BF16)
                packed[low, at] = (s_re * h_im + s_im * h_re).astype(BF16)
            return carry

        lax.fori_loop(0, lane_chunks, screen, 0)
        prod[0] = jnp.dot(packed[...], blk_ref[0], preferred_element_type=F32)
        prod[1] = jnp.dot(packed[...], blk_ref[1], preferred_element_type=F32)

        def unmix(n, carry):
            at = pl.ds(pl.multiple_of(n * LANES, LANES), LANES)
            values = []
            for k in range(groups):
                top = slice(k * part, (k + 1) * part)
                low = slice(half + k * part, half + (k + 1) * part)
                u_re = prod[0, top, at] + prod[1, low, at]
                u_im = prod[0, low, at] - prod[1, top, at]
                t_re = twist_ref[0, k : k + 1, at]
                t_im = twist_ref[1, k : k + 1, at]
                values.append(
                    (
                        (u_re * t_re + u_im * t_im).astype(BF16).astype(F32),
                        (u_im * t_re - u_re * t_im).astype(BF16).astype(F32),
                    )
                )
            for p, (re, im) in enumerate(small_dft(values, 1)):
                both = jnp.concatenate([re, im], 0) * (1.0 / total)
                send[slot_out, p, :, at] = both.astype(BF16)
            return carry

        lax.fori_loop(0, lane_chunks, unmix, 0)
        exchange(slot_out)

    def gather_part(slot, q, top, block=BLK):
        near = recv[slot].reshape(span, height)
        return jnp.dot(
            back_ref[pl.ds(top, block), q * span : (q + 1) * span],
            near,
            preferred_element_type=F32,
        )

    def spread(first, block, finish):
        for q in range(chunks - 1):
            arrive(first + q)

            def add(n, carry):
                top = pl.multiple_of(n * BLK, BLK)
                value = gather_part(first + q, q, top)
                at = pl.ds(top, BLK)
                acc[at, :] = value if q == 0 else acc[at, :] + value
                return carry

            lax.fori_loop(0, 2 * col_blocks, add, 0)
        q = chunks - 1
        arrive(first + q)

        for n in range(width // block):
            finish(n, functools.partial(result, first + q, q, block))

    def result(slot, q, block, n):
        top = pl.multiple_of(n * block, block)
        low = pl.multiple_of(width + n * block, block)
        re = gather_part(slot, q, top, block)
        im = gather_part(slot, q, low, block)
        if chunks > 1:
            re = re + acc[pl.ds(top, block), :]
            im = im + acc[pl.ds(low, block), :]
        return pl.ds(top, block), pl.ds(low, block), re * (1.0 / width), im * (1.0 / width)

    def weigh(n, made):
        top, low, re, im = made(n)
        residual = re * re + im * im - target_t[top, :]
        field[top, :] = (residual * re).astype(BF16)
        field[low, :] = (residual * im).astype(BF16)

    share = width // trials

    def hand_on(r):
        to = lax.rem(mine + r, trials)
        return pltpu.make_async_remote_copy(
            src_ref=gsend.at[to],
            dst_ref=grecv.at[r],
            send_sem=gsend_sem.at[r],
            recv_sem=grecv_sem.at[r],
            device_id=(to, me),
            device_id_type=MESH,
        )

    def slope(n, made):
        r = (n + 1) % trials
        to = lax.rem(mine + r, trials)
        top, low, re, im = made(to)
        value = 2.0 * (lens[top, :] * im - lens[low, :] * re)
        gsend[to] = value.astype(BF16)
        if r:
            hand_on(r).start()

    fetched("fwd")
    fetch("twist", twist_hbm, twist_ref, 1)
    fetch("target", target_hbm, target_ref, 4)
    fetch("blk", blk_hbm, blk_ref, 2)
    fetch("back", back_hbm, back_ref, 4)
    for q in range(chunks):
        columns(q, q)
        if q == 0:
            pl.semaphore_wait(barrier, groups + trials - 2)
        exchange(q)

    index_k = lax.broadcasted_iota(jnp.int32, (groups, height), 0)
    index_m = lax.broadcasted_iota(jnp.int32, (groups, height), 1)
    freq = index_k + groups * index_m
    signed = jnp.where(freq >= total // 2, freq - total, freq).astype(F32)
    r_cos, r_sin = cos_sin_pi((signed * signed) * (1.0 / total) * dist_ref[0])
    rowf[0] = r_cos
    rowf[1] = -r_sin

    def flip(b, carry):
        rows = pl.ds(pl.multiple_of((b % row_blocks) * BLK, BLK), BLK)
        cols = pl.ds(pl.multiple_of((b // row_blocks) * BLK, BLK), BLK)
        target_t[cols, rows] = target_ref[rows, cols].T
        return carry

    fetched("target")
    lax.fori_loop(0, row_blocks * col_blocks, flip, 0)
    fetched("twist")
    fetched("blk")

    for q in range(chunks):
        middle(q, chunks + q, q, False)
        if q == 0:
            fetched("back")
    spread(chunks, BLK, weigh)
    for q in range(chunks):
        columns(2 * chunks + q, q)
        exchange(2 * chunks + q)
    for q in range(chunks):
        middle(2 * chunks + q, 3 * chunks + q, q, True)
    spread(3 * chunks, share, slope)

    sum_all = gsend[mine].astype(F32)
    for r in range(1, trials):
        hand_on(r).wait_recv()
        sum_all = sum_all + grecv[r].astype(F32)
    out_ref[...] = sum_all

    for slot in range(4 * chunks):
        for r in range(1, groups):
            copy_to(slot, r).wait_send()
    for r in range(1, trials):
        hand_on(r).wait_send()


def local(phase_map, target, distance, etch_class, class_offset, aperture_start, aperture_stop):
    height, width = phase_map.shape
    kept = width // 2
    groups = lax.axis_size("row")
    trials = lax.axis_size("trial")
    slim = kept // groups
    chunks = 2 if slim % 16 == 0 and slim >= 32 else 1
    side = 2 * slim // chunks
    half = kept // chunks
    share = width // trials
    forward, backward, blk, twist = tables(height, width, kept, groups, chunks)
    smem = pl.BlockSpec(memory_space=pltpu.SMEM)
    hbm = pl.BlockSpec(memory_space=pltpu.HBM)
    vmem = pl.BlockSpec(memory_space=pltpu.VMEM)
    out = pl.pallas_call(
        functools.partial(kernel, (groups, trials, height, width, kept, chunks)),
        out_shape=jax.ShapeDtypeStruct((share, height), F32),
        in_specs=[smem] * 5 + [hbm] * 6,
        out_specs=vmem,
        scratch_shapes=[
            pltpu.VMEM(phase_map.shape, F32),
            pltpu.VMEM(target.shape, F32),
            pltpu.VMEM(forward.shape, BF16),
            pltpu.VMEM(backward.shape, BF16),
            pltpu.VMEM(blk.shape, BF16),
            pltpu.VMEM(twist.shape, F32),
            pltpu.SemaphoreType.DMA((height // BLK + 15,)),
            pltpu.VMEM((2 * width, height), F32),
            pltpu.VMEM((2 * width, height), BF16),
            pltpu.VMEM((width, height), F32),
            pltpu.VMEM((2, groups, height), F32),
            pltpu.VMEM((2 * width, height), F32),
            pltpu.VMEM((2 * half, height), BF16),
            pltpu.VMEM((2, 2 * half, height), F32),
            pltpu.VMEM((4 * chunks, groups, side, height), BF16),
            pltpu.VMEM((4 * chunks, groups, side, height), BF16),
            pltpu.VMEM((trials, share, height), BF16),
            pltpu.VMEM((trials, share, height), BF16),
            pltpu.SemaphoreType.DMA((4 * chunks, groups)),
            pltpu.SemaphoreType.DMA((4 * chunks, groups)),
            pltpu.SemaphoreType.DMA((trials,)),
            pltpu.SemaphoreType.DMA((trials,)),
        ],
        compiler_params=pltpu.CompilerParams(
            collective_id=0, has_side_effects=True, vmem_limit_bytes=67_043_328
        ),
    )(
        distance,
        etch_class,
        class_offset,
        aperture_start,
        aperture_stop,
        phase_map,
        target,
        forward,
        backward,
        blk,
        twist,
    )
    return out.T


def solution(mesh):
    return jax.shard_map(
        local,
        mesh=mesh,
        in_specs=(
            P("row", None),
            P("row", None),
            P("trial"),
            P("trial", "row", None),
            P(),
            P(),
            P(),
        ),
        out_specs=P("row", "trial"),
        check_vma=False,
    )
```

```python
import functools
import math

import jax
import jax.numpy as jnp
import numpy as np
from jax import lax
from jax.experimental import pallas as pl
from jax.experimental.pallas import tpu as pltpu
from jax.sharding import PartitionSpec as P

BLK = 128
LANES = 128
F32 = jnp.float32
BF16 = jnp.bfloat16
MESH = pl.DeviceIdType.MESH
MAGIC = 12582912.0


def even_fit(func, degree):
    cheb = np.polynomial.chebyshev.Chebyshev.interpolate(func, degree, domain=[0.0, 0.25])
    return [float(c) for c in cheb.convert(kind=np.polynomial.Polynomial).coef]


COS_FIT = even_fit(lambda z: np.cos(np.pi * np.sqrt(z)), 6)
SIN_FIT = even_fit(lambda z: np.pi * np.sinc(np.sqrt(z)), 5)


def horner(coefs, z):
    total = jnp.full_like(z, coefs[-1])
    for c in coefs[-2::-1]:
        total = total * z + c
    return total


def nearest(u):
    return (u + MAGIC) - MAGIC


def turn(u):
    whole = nearest(u)
    rest = u - whole
    z = rest * rest
    return horner(COS_FIT, z), rest * horner(SIN_FIT, z), whole


def cos_sin_pi(u):
    cos, sin, whole = turn(u)
    half = whole * 0.5
    odd = half - nearest(half)
    sign = 1.0 - 8.0 * (odd * odd)
    return cos * sign, sin * sign


def scale_turn(re, im, k, n, sign):
    if k == 0:
        return re, im
    if 4 * k == n:
        return (-im, re) if sign > 0 else (im, -re)
    c = math.cos(2 * math.pi * k / n)
    s = sign * math.sin(2 * math.pi * k / n)
    if 8 * k == n:
        return ((re - im) * c, (re + im) * c) if sign > 0 else ((re + im) * c, (im - re) * c)
    return re * c - im * s, re * s + im * c


def small_dft(values, sign):
    n = len(values)
    if n == 1:
        return values
    even = small_dft(values[0::2], sign)
    odd = small_dft(values[1::2], sign)
    low, high = [], []
    for k in range(n // 2):
        re, im = scale_turn(*odd[k], k, n, sign)
        low.append((even[k][0] + re, even[k][1] + im))
        high.append((even[k][0] - re, even[k][1] - im))
    return low + high


def tables(height, width, kept, groups, chunks):
    slim = kept // groups
    part = slim // chunks
    cols = np.arange(width)
    freqs = np.arange(kept) - kept // 2
    angle = -2.0 * np.pi / width * np.mod(cols[:, None] * freqs[None, :], width)
    re = np.cos(angle).T.reshape(groups, chunks, part, width)
    im = np.sin(angle).T.reshape(groups, chunks, part, width)
    rows_re = np.concatenate([re, -im], 3)
    rows_im = np.concatenate([im, re], 3)
    forward = np.stack([rows_re, rows_im], 2)
    forward = forward.transpose(1, 0, 2, 3, 4).reshape(2 * kept, 2 * width)
    places = np.arange(height)
    angle = -2.0 * np.pi / height * np.mod(places[:, None] * places[None, :], height)
    blk = np.stack([np.cos(angle), np.sin(angle)])
    total = height * groups
    angle = -2.0 * np.pi / total * np.mod(np.arange(groups)[:, None] * places[None, :], total)
    twist = np.stack([np.cos(angle), np.sin(angle)])
    as_bf16 = lambda a: jnp.asarray(a.astype(np.float32).astype(BF16))
    return as_bf16(forward), as_bf16(forward.T), as_bf16(blk), jnp.asarray(twist.astype(np.float32))


def kernel(
    dims,
    dist_ref,
    class_ref,
    level_ref,
    start_ref,
    stop_ref,
    phase_hbm,
    target_hbm,
    fwd_hbm,
    back_hbm,
    blk_hbm,
    twist_hbm,
    out_ref,
    phase_ref,
    target_ref,
    fwd_ref,
    back_ref,
    blk_ref,
    twist_ref,
    fetch_sem,
    lens,
    field,
    target_t,
    rowf,
    acc,
    packed,
    prod,
    send,
    recv,
    gsend,
    grecv,
    send_sem,
    recv_sem,
    gsend_sem,
    grecv_sem,
):
    groups, trials, height, width, kept, chunks = dims
    slim = kept // groups
    part = slim // chunks
    side = 2 * part
    half = groups * part
    span = 2 * kept // chunks
    total = height * groups
    me = lax.axis_index("row")
    mine = lax.axis_index("trial")
    lane_chunks = height // LANES

    fetches = {}

    def fetch(name, source, dest, pieces):
        rows = source.shape[0] // pieces
        made = []
        for n in range(pieces):
            at = pl.ds(n * rows, rows)
            place = sum(len(c) for c in fetches.values()) + n
            made.append(
                pltpu.make_async_copy(source.at[at], dest.at[at], fetch_sem.at[place])
            )
            made[-1].start()
        fetches[name] = made

    def fetched(name):
        for made in fetches[name]:
            made.wait()

    fetch("phase", phase_hbm, phase_ref, height // BLK)
    fetch("fwd", fwd_hbm, fwd_ref, 4)

    barrier = pltpu.get_barrier_semaphore()
    for r in range(1, groups):
        pl.semaphore_signal(
            barrier, inc=1, device_id=(mine, lax.rem(me + r, groups)), device_id_type=MESH
        )
    for r in range(1, trials):
        pl.semaphore_signal(
            barrier, inc=1, device_id=(lax.rem(mine + r, trials), me), device_id_type=MESH
        )

    row_blocks = height // BLK
    col_blocks = width // BLK

    def lens_block(rb, cb, carry):
        rows = pl.ds(rb * BLK, BLK)
        cols = pl.ds(pl.multiple_of(cb * BLK, BLK), BLK)
        offset = level_ref[class_ref[0, rb, cb]]
        where = me * row_blocks + rb
        inside = jnp.where(
            jnp.logical_and(where >= start_ref[cb], where < stop_ref[cb]), 1.0, 0.0
        ).astype(F32)
        angle = phase_ref[rows, cols].T + offset
        cos, sin, whole = turn(angle * (1.0 / math.pi))
        sign = inside - (2.0 * inside) * (whole * whole)
        re = cos * sign
        im = sin * sign
        low = pl.ds(pl.multiple_of(width + cb * BLK, BLK), BLK)
        lens[cols, rows] = re
        lens[low, rows] = im
        field[cols, rows] = re.astype(BF16)
        field[low, rows] = im.astype(BF16)
        return carry

    for rb in range(row_blocks):
        fetches["phase"][rb].wait()
        lax.fori_loop(0, col_blocks, functools.partial(lens_block, rb), 0)

    def copy_to(slot, r):
        to = lax.rem(me + r, groups)
        return pltpu.make_async_remote_copy(
            src_ref=send.at[slot, to],
            dst_ref=recv.at[slot, me],
            send_sem=send_sem.at[slot, r],
            recv_sem=recv_sem.at[slot, r],
            device_id=(mine, to),
            device_id_type=MESH,
        )

    def exchange(slot):
        for r in sorted(range(1, groups), key=lambda r: min(r, groups - r)):
            copy_to(slot, r).start()
        recv[slot, me] = send[slot, me]

    def arrive(slot):
        for r in range(1, groups):
            copy_to(slot, r).wait_recv()

    def columns(slot, q):
        made = jnp.dot(
            fwd_ref[q * span : (q + 1) * span, :], field[...], preferred_element_type=F32
        )
        send[slot] = made.astype(BF16).reshape(groups, side, height)

    def middle(slot_in, slot_out, q, conj):
        arrive(slot_in)

        def mix(n, carry):
            at = pl.ds(pl.multiple_of(n * LANES, LANES), LANES)
            values = []
            for p in range(groups):
                both = recv[slot_in, p, :, at].astype(F32)
                values.append((both[:part], both[part:]))
            for k, (re, im) in enumerate(small_dft(values, -1)):
                t_re = twist_ref[0, k : k + 1, at]
                t_im = twist_ref[1, k : k + 1, at]
                packed[k * part : (k + 1) * part, at] = (re * t_re - im * t_im).astype(BF16)
                packed[half + k * part : half + (k + 1) * part, at] = (
                    re * t_im + im * t_re
                ).astype(BF16)
            return carry

        lax.fori_loop(0, lane_chunks, mix, 0)
        prod[0] = jnp.dot(packed[...], blk_ref[0], preferred_element_type=F32)
        prod[1] = jnp.dot(packed[...], blk_ref[1], preferred_element_type=F32)
        across = (
            lax.broadcasted_iota(jnp.int32, (part, LANES), 0)
            + (me * slim + q * part - kept // 2)
        ).astype(F32)
        c_re, c_im = cos_sin_pi(
            (across * across) * (total / (width * width)) * dist_ref[0]
        )
        c_im = -c_im

        def screen(n, carry):
            at = pl.ds(pl.multiple_of(n * LANES, LANES), LANES)
            for k in range(groups):
                top = slice(k * part, (k + 1) * part)
                low = slice(half + k * part, half + (k + 1) * part)
                s_re = prod[0, top, at] - prod[1, low, at]
                s_im = prod[1, top, at] + prod[0, low, at]
                r_re = rowf[0, k : k + 1, at]
                r_im = rowf[1, k : k + 1, at]
                h_re = r_re * c_re - r_im * c_im
                h_im = r_re * c_im + r_im * c_re
                if conj:
                    h_im = -h_im
                packed[top, at] = (s_re * h_re - s_im * h_im).astype(BF16)
                packed[low, at] = (s_re * h_im + s_im * h_re).astype(BF16)
            return carry

        lax.fori_loop(0, lane_chunks, screen, 0)
        prod[0] = jnp.dot(packed[...], blk_ref[0], preferred_element_type=F32)
        prod[1] = jnp.dot(packed[...], blk_ref[1], preferred_element_type=F32)

        def unmix(n, carry):
            at = pl.ds(pl.multiple_of(n * LANES, LANES), LANES)
            values = []
            for k in range(groups):
                top = slice(k * part, (k + 1) * part)
                low = slice(half + k * part, half + (k + 1) * part)
                u_re = prod[0, top, at] + prod[1, low, at]
                u_im = prod[0, low, at] - prod[1, top, at]
                t_re = twist_ref[0, k : k + 1, at]
                t_im = twist_ref[1, k : k + 1, at]
                values.append(
                    (
                        (u_re * t_re + u_im * t_im).astype(BF16).astype(F32),
                        (u_im * t_re - u_re * t_im).astype(BF16).astype(F32),
                    )
                )
            for p, (re, im) in enumerate(small_dft(values, 1)):
                both = jnp.concatenate([re, im], 0) * (1.0 / total)
                send[slot_out, p, :, at] = both.astype(BF16)
            return carry

        lax.fori_loop(0, lane_chunks, unmix, 0)
        exchange(slot_out)

    def gather_part(slot, q, top, block=BLK):
        near = recv[slot].reshape(span, height)
        return jnp.dot(
            back_ref[pl.ds(top, block), q * span : (q + 1) * span],
            near,
            preferred_element_type=F32,
        )

    def spread(first, block, finish):
        for q in range(chunks - 1):
            arrive(first + q)

            def add(n, carry):
                top = pl.multiple_of(n * BLK, BLK)
                value = gather_part(first + q, q, top)
                at = pl.ds(top, BLK)
                acc[at, :] = value if q == 0 else acc[at, :] + value
                return carry

            lax.fori_loop(0, 2 * col_blocks, add, 0)
        q = chunks - 1
        arrive(first + q)

        for n in range(width // block):
            finish(n, functools.partial(result, first + q, q, block))

    def result(slot, q, block, n):
        top = pl.multiple_of(n * block, block)
        low = pl.multiple_of(width + n * block, block)
        re = gather_part(slot, q, top, block)
        im = gather_part(slot, q, low, block)
        if chunks > 1:
            re = re + acc[pl.ds(top, block), :]
            im = im + acc[pl.ds(low, block), :]
        return pl.ds(top, block), pl.ds(low, block), re * (1.0 / width), im * (1.0 / width)

    def weigh(n, made):
        top, low, re, im = made(n)
        residual = re * re + im * im - target_t[top, :]
        field[top, :] = (residual * re).astype(BF16)
        field[low, :] = (residual * im).astype(BF16)

    share = width // trials

    def hand_on(r):
        to = lax.rem(mine + r, trials)
        return pltpu.make_async_remote_copy(
            src_ref=gsend.at[to],
            dst_ref=grecv.at[r],
            send_sem=gsend_sem.at[r],
            recv_sem=grecv_sem.at[r],
            device_id=(to, me),
            device_id_type=MESH,
        )

    def slope(n, made):
        r = (n + 1) % trials
        to = lax.rem(mine + r, trials)
        top, low, re, im = made(to)
        value = 2.0 * (lens[top, :] * im - lens[low, :] * re)
        gsend[to] = value.astype(BF16)
        if r:
            hand_on(r).start()

    fetched("fwd")
    fetch("twist", twist_hbm, twist_ref, 1)
    fetch("target", target_hbm, target_ref, 4)
    fetch("blk", blk_hbm, blk_ref, 2)
    fetch("back", back_hbm, back_ref, 4)
    for q in range(chunks):
        columns(q, q)
        if q == 0:
            pl.semaphore_wait(barrier, groups + trials - 2)
        exchange(q)

    index_k = lax.broadcasted_iota(jnp.int32, (groups, height), 0)
    index_m = lax.broadcasted_iota(jnp.int32, (groups, height), 1)
    freq = index_k + groups * index_m
    signed = jnp.where(freq >= total // 2, freq - total, freq).astype(F32)
    r_cos, r_sin = cos_sin_pi((signed * signed) * (1.0 / total) * dist_ref[0])
    rowf[0] = r_cos
    rowf[1] = -r_sin

    def flip(b, carry):
        rows = pl.ds(pl.multiple_of((b % row_blocks) * BLK, BLK), BLK)
        cols = pl.ds(pl.multiple_of((b // row_blocks) * BLK, BLK), BLK)
        target_t[cols, rows] = target_ref[rows, cols].T
        return carry

    fetched("target")
    lax.fori_loop(0, row_blocks * col_blocks, flip, 0)
    fetched("twist")
    fetched("blk")

    for q in range(chunks):
        middle(q, chunks + q, q, False)
        if q == 0:
            fetched("back")
    spread(chunks, BLK, weigh)
    for q in range(chunks):
        columns(2 * chunks + q, q)
        exchange(2 * chunks + q)
    for q in range(chunks):
        middle(2 * chunks + q, 3 * chunks + q, q, True)
    spread(3 * chunks, share, slope)

    sum_all = gsend[mine].astype(F32)
    for r in range(1, trials):
        hand_on(r).wait_recv()
        sum_all = sum_all + grecv[r].astype(F32)
    out_ref[...] = sum_all

    for slot in range(4 * chunks):
        for r in range(1, groups):
            copy_to(slot, r).wait_send()
    for r in range(1, trials):
        hand_on(r).wait_send()


def local(phase_map, target, distance, etch_class, class_offset, aperture_start, aperture_stop):
    height, width = phase_map.shape
    kept = width // 2
    groups = lax.axis_size("row")
    trials = lax.axis_size("trial")
    slim = kept // groups
    chunks = 2 if slim % 16 == 0 and slim >= 32 else 1
    side = 2 * slim // chunks
    half = kept // chunks
    share = width // trials
    forward, backward, blk, twist = tables(height, width, kept, groups, chunks)
    smem = pl.BlockSpec(memory_space=pltpu.SMEM)
    hbm = pl.BlockSpec(memory_space=pltpu.HBM)
    vmem = pl.BlockSpec(memory_space=pltpu.VMEM)
    out = pl.pallas_call(
        functools.partial(kernel, (groups, trials, height, width, kept, chunks)),
        out_shape=jax.ShapeDtypeStruct((share, height), F32),
        in_specs=[smem] * 5 + [hbm] * 6,
        out_specs=vmem,
        scratch_shapes=[
            pltpu.VMEM(phase_map.shape, F32),
            pltpu.VMEM(target.shape, F32),
            pltpu.VMEM(forward.shape, BF16),
            pltpu.VMEM(backward.shape, BF16),
            pltpu.VMEM(blk.shape, BF16),
            pltpu.VMEM(twist.shape, F32),
            pltpu.SemaphoreType.DMA((height // BLK + 15,)),
            pltpu.VMEM((2 * width, height), F32),
            pltpu.VMEM((2 * width, height), BF16),
            pltpu.VMEM((width, height), F32),
            pltpu.VMEM((2, groups, height), F32),
            pltpu.VMEM((2 * width, height), F32),
            pltpu.VMEM((2 * half, height), BF16),
            pltpu.VMEM((2, 2 * half, height), F32),
            pltpu.VMEM((4 * chunks, groups, side, height), BF16),
            pltpu.VMEM((4 * chunks, groups, side, height), BF16),
            pltpu.VMEM((trials, share, height), BF16),
            pltpu.VMEM((trials, share, height), BF16),
            pltpu.SemaphoreType.DMA((4 * chunks, groups)),
            pltpu.SemaphoreType.DMA((4 * chunks, groups)),
            pltpu.SemaphoreType.DMA((trials,)),
            pltpu.SemaphoreType.DMA((trials,)),
        ],
        compiler_params=pltpu.CompilerParams(
            collective_id=0, has_side_effects=True, vmem_limit_bytes=67_043_328
        ),
    )(
        distance,
        etch_class,
        class_offset,
        aperture_start,
        aperture_stop,
        phase_map,
        target,
        forward,
        backward,
        blk,
        twist,
    )
    return out.T


def solution(mesh):
    return jax.shard_map(
        local,
        mesh=mesh,
        in_specs=(
            P("row", None),
            P("row", None),
            P("trial"),
            P("trial", "row", None),
            P(),
            P(),
            P(),
        ),
        out_specs=P("row", "trial"),
        check_vma=False,
    )
```
